32 devices in a mesh: groups: 2 (over x), ctx: 16 (over z, y, core).
Axes of the slice: x: 2, y: 2, z: 4, core: 2. Of those that a mesh axis runs over, the one named last changes fastest.
Arguments:
- frames: bfloat16 [32, 384, 1024], P('groups', 'ctx'), parts along dimension 0, may hold values from -6 to 6
- grad_out: bfloat16 [12288, 1024], P(('groups', 'ctx')), parts along dimension 0, may hold values from -6 to 6
- valid_count: int32 [2], P('groups'), parts along dimension 0, may hold values from 3072 to 6144
- norm_gain: float32 [1024], replicated, may hold values from 0.1 to 1.9
- w_in: bfloat16 [2048, 1024], P('ctx'), may hold values from -0.1875 to 0.1875
- depth_weight: bfloat16 [1024, 31], replicated, may hold values from -1 to 1
- depth_gain: float32 [1024], replicated, may hold values from 0.1 to 1.9
- w_out: bfloat16 [1024, 1024], P('ctx'), may hold values from -0.1875 to 0.1875
Outputs:
- output: bfloat16 [12288, 1024], P(('groups', 'ctx')), parts along dimension 0
- grad_frames: bfloat16 [32, 384, 1024], P('groups', 'ctx'), parts along dimension 0
- grad_w_in: float32 [4096, 1024], P(('groups', 'ctx')), parts along dimension 0
- grad_w_out: float32 [2048, 1024], P(('groups', 'ctx')), parts along dimension 0
- grad_depth: float32 [2048, 31], P('groups'), parts along dimension 0
- grad_gains: float32 [4, 1024], P('groups'), parts along dimension 0
The draws below stay inside these ranges and needn't reach their ends.
There are 2 independent parts, one for each index of `groups`. The reference program is written for one: setup_inputs(seed, part) draws one part's arguments, and reference() takes and returns one part's arrays. A program takes and returns all parts, laid end to end along the dimension named above; an argument that names none is the same for every part. Nothing has to cross between parts.
Inputs may be any that keep to these rules, and one draw needn't show every extreme that they name: frames from index valid_count[0] on are padding.
All inputs are finite; a program needn't handle non-finite values.
Results may differ from the reference program's by a relative error of at most 0.0069.
Values may be sent and summed in bfloat16 or wider, within the bound.
A program may use at most 128 MiB of HBM per device.

```python
import jax
import jax.numpy as jnp
from jax import lax

D = 1024
K = 31
TOK_DEV = 384
BLOCKS = 16
TOKENS = 6144


def raised(result, own_key, source, target, parts, factor):
    owner, partner = [(jnp.arange(result.shape[dim]) // (result.shape[dim] // parts)).reshape([-1 if axis == dim else 1 for axis in range(result.ndim)]) for dim in (source, target)]
    chosen = jax.random.permutation(own_key, parts)[partner]
    strong = (owner == chosen) | (owner == (partner + parts // 2) % parts)
    return jnp.where(strong, factor * result, result)


def levels(own_key, dims, cuts, smallest, high):
    factor_of = 1.0
    for position, shards_of in cuts:
        draws = jax.random.uniform(jax.random.fold_in(jax.random.fold_in(own_key, 6), position), (shards_of,), jnp.float32, smallest / len(cuts), high / len(cuts))
        factor_of = factor_of * jnp.repeat(jnp.exp(draws), dims[position] // shards_of).reshape((-1,) + (1,) * (len(dims) - 1 - position))
    return factor_of


def noise(key, shape, scale, reach, pieces=(), kind=jnp.bfloat16):
    result = jax.random.normal(key, shape, jnp.float32) * scale
    if len(pieces) > 0:
        result = levels(key, shape, pieces, -0.22, 0.18) * result
    return jnp.clip(result, min=-reach, max=reach).astype(kind)


def heavy_noise(own_key, extent, scale, bound, shards, heavy, kind=jnp.bfloat16):
    result = scale * jax.random.normal(own_key, extent, jnp.float32)
    if shards:
        result = result * levels(own_key, extent, shards, -0.22, 0.18)
    return jnp.clip(raised(result, jax.random.fold_in(own_key, 3), *heavy), -bound, bound).astype(kind)


def setup_inputs(seed: int = 0, part: int = 0) -> dict:
    arg_keys = jax.random.split(jax.random.key(seed), 9)
    part_splits = jax.random.split(jax.random.fold_in(arg_keys[8], part), 9)
    frames = noise(part_splits[0], (BLOCKS, TOK_DEV, D), 1.0, 6.0, ((1, 16),))
    grad_out = heavy_noise(part_splits[1], (TOKENS, D), 1.0, 6.0, ((0, 16),), (0, 1, 16, 2.0))
    valid_count = jax.random.randint(part_splits[2], (1,), TOKENS // 2, TOKENS + 1).astype(jnp.int32)
    norm_gain = jnp.clip(1.0 + 0.18 * jax.random.normal(arg_keys[3], (D,), jnp.float32), 0.1, 1.9)
    w_in = noise(arg_keys[4], (2 * D, D), D ** -0.5, 0.1875, ((0, 16),))
    depth_weight = noise(arg_keys[5], (D, K), K ** -0.5, 1.0)
    depth_gain = jnp.clip(1.0 + 0.18 * jax.random.normal(arg_keys[6], (D,), jnp.float32), 0.1, 1.9)
    w_out = noise(arg_keys[7], (D, D), D ** -0.5, 0.1875, ((0, 16),))
    return {"frames": frames, "grad_out": grad_out, "valid_count": valid_count, "norm_gain": norm_gain, "w_in": w_in, "depth_weight": depth_weight, "depth_gain": depth_gain, "w_out": w_out}


epsilon = 1e-05

def normalize(values):
    center = lax.optimization_barrier(jnp.mean(values, axis=-1, keepdims=True))
    shifted = values - center
    inverse = lax.rsqrt(lax.optimization_barrier(jnp.mean(shifted * shifted, axis=-1, keepdims=True)) + epsilon)
    return (shifted * inverse, inverse)

def norm_backward(upstream, normed, inverse):
    first = lax.optimization_barrier(jnp.mean(upstream, axis=-1, keepdims=True))
    second = lax.optimization_barrier(jnp.mean(upstream * normed, axis=-1, keepdims=True))
    return (upstream - first - normed * second) * inverse

def frame_sum(left, right):
    return lax.dot_general(left, right, (((0,), (0,)), ((), ())), preferred_element_type=jnp.float32)

def times_transposed(left, right):
    return lax.dot_general(left, right, (((1,), (1,)), ((), ())), preferred_element_type=jnp.float32)

def depthwise(padded, kernel, length):
    total = padded[0:length] * kernel[:, 0]
    for offset in range(1, kernel.shape[1]):
        total = total + padded[offset:offset + length] * kernel[:, offset]
    return total

def depthwise_back(padded, kernel, length):
    taps = kernel.shape[1]
    total = padded[taps - 1:taps - 1 + length] * kernel[:, 0]
    for offset in range(1, taps):
        begin = taps - 1 - offset
        total = total + padded[begin:begin + length] * kernel[:, offset]
    return total

def reference(frames, grad_out, valid_count, norm_gain, w_in, depth_weight, depth_gain, w_out):
    length = frames.shape[0] * frames.shape[1]
    width = frames.shape[2]
    taps = depth_weight.shape[1]
    margin = (taps - 1) // 2
    scale = length ** (-0.5)
    inputs = frames.reshape(length, width)
    wide_in = inputs.astype(jnp.float32)
    normed_in, inverse_in = normalize(wide_in)
    scaled_in = (normed_in * norm_gain).astype(jnp.bfloat16)
    projected = times_transposed(scaled_in, w_in)
    linear = projected[:, :width]
    sigma = jax.nn.sigmoid(projected[:, width:])
    keep = (jnp.arange(length, dtype=jnp.int32) < valid_count[0]).astype(jnp.float32)[:, None]
    glu = (linear * sigma * keep).astype(jnp.bfloat16)
    padded = jnp.pad(glu, ((margin, margin), (0, 0))).astype(jnp.float32)
    kernel = depth_weight.astype(jnp.float32)
    conv = depthwise(padded, kernel, length)
    normed_conv, inverse_conv = normalize(conv)
    gained = normed_conv * depth_gain
    sig_two = jax.nn.sigmoid(gained)
    act = (gained * sig_two * keep).astype(jnp.bfloat16)
    output = (wide_in + times_transposed(act, w_out)).astype(jnp.bfloat16)
    grad_w_out = frame_sum(grad_out, act) * scale
    grad_act = jnp.dot(grad_out, w_out, preferred_element_type=jnp.float32)
    grad_gained = grad_act * keep * (sig_two * (1.0 + gained * (1.0 - sig_two)))
    grad_conv = norm_backward(grad_gained * depth_gain, normed_conv, inverse_conv).astype(jnp.bfloat16)
    grad_pad = jnp.pad(grad_conv, ((margin, margin), (0, 0))).astype(jnp.float32)
    grad_glu = depthwise_back(grad_pad, kernel, length) * keep
    grad_wide = grad_conv.astype(jnp.float32)
    grad_depth = jnp.stack([lax.optimization_barrier(jnp.sum(grad_wide * padded[offset:offset + length], axis=0)) for offset in range(taps)], axis=1) * scale
    grad_projected = jnp.concatenate([grad_glu * sigma, grad_glu * linear * sigma * (1.0 - sigma)], axis=1).astype(jnp.bfloat16)
    grad_w_in = frame_sum(grad_projected, scaled_in) * scale
    grad_scaled = jnp.dot(grad_projected, w_in, preferred_element_type=jnp.float32)
    grad_in = norm_backward(grad_scaled * norm_gain, normed_in, inverse_in)
    grad_gains = jnp.stack([lax.optimization_barrier(jnp.sum(grad_scaled * normed_in, axis=0)), lax.optimization_barrier(jnp.sum(grad_gained * normed_conv, axis=0))], axis=0) * scale
    grad_frames = (grad_out.astype(jnp.float32) + grad_in).astype(jnp.bfloat16).reshape(frames.shape)
    return (output, grad_frames, grad_w_in, grad_w_out, grad_depth, grad_gains)
```

```python
import functools

import jax
import jax.numpy as jnp
from jax import lax
from jax.experimental import pallas as pl
from jax.experimental.pallas import tpu as pltpu
from jax.sharding import PartitionSpec as P

MESH = pl.DeviceIdType.MESH

epsilon = 1e-05


def extended(block, sides, width):
    for axis, dim in sides:
        count = lax.axis_size(axis)
        forward = [(i, i + 1) for i in range(count - 1)]
        backward = [(target, source) for source, target in forward]
        low = lax.ppermute(
            lax.slice_in_dim(block, block.shape[dim] - width, None, axis=dim), axis, forward
        )
        high = lax.ppermute(lax.slice_in_dim(block, 0, width, axis=dim), axis, backward)
        block = jnp.concatenate([low, block, high], axis=dim)
    return block


def normalize(values):
    center = jnp.mean(values, axis=-1, keepdims=True)
    shifted = values - center
    inverse = lax.rsqrt(jnp.mean(shifted * shifted, axis=-1, keepdims=True) + epsilon)
    return (shifted * inverse, inverse)


def norm_backward(upstream, normed, inverse):
    first = jnp.mean(upstream, axis=-1, keepdims=True)
    second = jnp.mean(upstream * normed, axis=-1, keepdims=True)
    return (upstream - first - normed * second) * inverse


def frame_sum(left, right):
    return lax.dot_general(
        left, right, (((0,), (0,)), ((), ())), preferred_element_type=jnp.float32
    )


def times_transposed(left, right):
    return lax.dot_general(
        left, right, (((1,), (1,)), ((), ())), preferred_element_type=jnp.float32
    )


def depthwise(padded, kernel, length):
    total = padded[0:length] * kernel[:, 0]
    for offset in range(1, kernel.shape[1]):
        total = total + padded[offset : offset + length] * kernel[:, offset]
    return total


def depthwise_back(padded, kernel, length):
    taps = kernel.shape[1]
    total = padded[taps - 1 : taps - 1 + length] * kernel[:, 0]
    for offset in range(1, taps):
        begin = taps - 1 - offset
        total = total + padded[begin : begin + length] * kernel[:, offset]
    return total


def grid_of(chips):
    columns = 2 ** ((chips.bit_length() - 1) // 2)
    return (chips // columns, columns)


def chip_at(place, chips):
    rows, columns = grid_of(chips)
    inner = columns - 1
    step = jnp.maximum(place - 1, 0)
    row = lax.div(step, inner)
    column = lax.rem(step, inner)
    column = jnp.where(lax.rem(row, 2) == 0, column, inner - 1 - column)
    snake = row * columns + 1 + column
    back = lax.rem(chips - place, chips) * columns
    return jnp.where((place >= 1) & (place <= rows * inner), snake, back)


def place_of(chip, chips):
    rows, columns = grid_of(chips)
    inner = columns - 1
    row = lax.div(chip, columns)
    column = lax.rem(chip, columns) - 1
    turned = jnp.where(lax.rem(row, 2) == 0, column, inner - 1 - column)
    return jnp.where(column < 0, lax.rem(chips - row, chips), row * inner + turned + 1)


def position(chips):
    me = lax.axis_index("ctx")
    core = lax.rem(me, 2)
    place = place_of(lax.div(me, 2), chips)
    right = chip_at(lax.rem(place + 1, chips), chips) * 2 + core
    left = chip_at(lax.rem(place + chips - 1, chips), chips) * 2 + core
    return (place, core, me + 1 - 2 * core, right, left)


def greet(devices):
    barrier = pltpu.get_barrier_semaphore()
    for device in devices:
        pl.semaphore_signal(barrier, inc=1, device_id={"ctx": device}, device_id_type=MESH)
    pl.semaphore_wait(barrier, len(devices))


def reduce_kernel(
    chips, first_ref, second_ref, first_out, second_out, outgoing, incoming, held, *sems
):
    swap_send, swap_recv, ring_send, ring_recv = sems
    place, core, partner, right, left = position(chips)
    upper = first_ref.shape[2]
    rows = upper + second_ref.shape[2]
    half = first_ref.shape[3] // 2
    parts = ((first_ref, first_out, 0, upper), (second_ref, second_out, upper, rows))
    greet((partner, right, left))

    def owner(way, step):
        ahead = place + 1 + step if way else place + 2 * chips - 1 - step
        return chip_at(lax.rem(ahead, chips), chips)

    def swap(step):
        return pltpu.make_async_remote_copy(
            src_ref=outgoing.at[step],
            dst_ref=incoming.at[step],
            send_sem=swap_send.at[step],
            recv_sem=swap_recv.at[step],
            device_id={"ctx": partner},
            device_id_type=MESH,
        )

    def hop(way, step):
        return pltpu.make_async_remote_copy(
            src_ref=held.at[way, step],
            dst_ref=held.at[way, step + 1],
            send_sem=ring_send.at[way, step],
            recv_sem=ring_recv.at[way, step],
            device_id={"ctx": left if way else right},
            device_id_type=MESH,
        )

    def give(step, carry):
        for way in range(2):
            columns = slice(way * half, (way + 1) * half)
            chip = owner(way, step)
            for source, _, begin, end in parts:
                outgoing[step, begin:end, columns] = source[chip, 1 - core, :, columns]
        swap(step).start()
        return carry

    def total(way, step, part, arrived):
        source, _, begin, end = part
        columns = slice(way * half, (way + 1) * half)
        value = source[owner(way, step), core, :, columns].astype(jnp.float32)
        value = value + incoming[step, begin:end, columns].astype(jnp.float32)
        if arrived:
            value = value + held[way, step, begin:end, :].astype(jnp.float32)
        return value

    def move(step, arrived):
        swap(step).wait_recv()
        for way in range(2):
            if arrived:
                hop(way, step - 1).wait_recv()
            for part in parts:
                held[way, step, part[2] : part[3], :] = total(way, step, part, arrived).astype(
                    held.dtype
                )
            hop(way, step).start()

    lax.fori_loop(0, chips, give, 0)
    move(0, False)

    def middle(step, carry):
        move(step, True)
        return carry

    lax.fori_loop(1, chips - 1, middle, 0)
    swap(chips - 1).wait_recv()
    for way in range(2):
        hop(way, chips - 2).wait_recv()
        for part in parts:
            part[1][:, way * half : (way + 1) * half] = total(way, chips - 1, part, True)

    def drain(step, carry):
        swap(step).wait_send()
        for way in range(2):
            hop(way, step).wait_send()
        return carry

    lax.fori_loop(0, chips - 1, drain, 0)
    swap(chips - 1).wait_send()


def reduce_rows(first, second, span):
    chips = span // 2
    width = first.shape[1]
    upper, lower = first.shape[0] // span, second.shape[0] // span
    rows = upper + lower
    whole = pl.BlockSpec(memory_space=pltpu.VMEM)
    return pl.pallas_call(
        functools.partial(reduce_kernel, chips),
        out_shape=(
            jax.ShapeDtypeStruct((upper, width), jnp.float32),
            jax.ShapeDtypeStruct((lower, width), jnp.float32),
        ),
        in_specs=[whole] * 2,
        out_specs=(whole,) * 2,
        scratch_shapes=[
            pltpu.VMEM((chips, rows, width), first.dtype),
            pltpu.VMEM((chips, rows, width), first.dtype),
            pltpu.VMEM((2, chips, rows, width // 2), first.dtype),
            pltpu.SemaphoreType.DMA((chips,)),
            pltpu.SemaphoreType.DMA((chips,)),
            pltpu.SemaphoreType.DMA((2, chips - 1)),
            pltpu.SemaphoreType.DMA((2, chips - 1)),
        ],
        compiler_params=pltpu.CompilerParams(
            collective_id=0, has_side_effects=True, vmem_limit_bytes=44 * 2**20
        ),
        cost_estimate=pl.CostEstimate(flops=10**7, bytes_accessed=120 * 10**6, transcendentals=0),
        name="reduce_rows",
    )(first.reshape(chips, 2, upper, width), second.reshape(chips, 2, lower, width))


def shards(frames, grad_out, valid_count, norm_gain, w_in, depth_weight, depth_gain, w_out):
    span = lax.axis_size("ctx")
    ordered = lax.all_to_all(frames, "ctx", split_axis=0, concat_axis=1, tiled=True)
    local_frames = ordered.shape[1]
    width = ordered.shape[2]
    taps = depth_weight.shape[1]
    margin = (taps - 1) // 2
    scale = (local_frames * span) ** (-0.5)
    inputs = ordered.reshape(local_frames, width)
    positions = lax.axis_index("ctx") * local_frames + lax.iota(jnp.int32, local_frames)
    keep = (positions < valid_count[0]).astype(jnp.float32)[:, None]
    wide_in = inputs.astype(jnp.float32)
    normed_in, inverse_in = normalize(wide_in)
    scaled_in = (normed_in * norm_gain).astype(jnp.bfloat16)
    projected = times_transposed(scaled_in, lax.all_gather(w_in, "ctx", axis=0, tiled=True))
    linear = projected[:, :width]
    sigma = jax.nn.sigmoid(projected[:, width:])
    glu = (linear * sigma * keep).astype(jnp.bfloat16)
    padded = extended(glu, (("ctx", 0),), margin).astype(jnp.float32)
    kernel = depth_weight.astype(jnp.float32)
    conv = depthwise(padded, kernel, local_frames)
    normed_conv, inverse_conv = normalize(conv)
    gained = normed_conv * depth_gain
    sig_two = jax.nn.sigmoid(gained)
    act = (gained * sig_two * keep).astype(jnp.bfloat16)
    mixed = times_transposed(act, lax.all_gather(w_out, "ctx", axis=0, tiled=True))
    output = (wide_in + mixed).astype(jnp.bfloat16)
    sent = jnp.bfloat16 if span <= 32 else jnp.float32
    partial_out = frame_sum(grad_out, act).astype(sent)
    columns = grad_out
    grad_act = jnp.dot(
        columns,
        lax.all_gather(w_out, "ctx", axis=0, tiled=True),
        preferred_element_type=jnp.float32,
    )
    grad_gained = grad_act * keep * (sig_two * (1.0 + gained * (1.0 - sig_two)))
    grad_conv = norm_backward(grad_gained * depth_gain, normed_conv, inverse_conv).astype(
        jnp.bfloat16
    )
    grad_pad = extended(grad_conv, (("ctx", 0),), margin).astype(jnp.float32)
    grad_glu = depthwise_back(grad_pad, kernel, local_frames) * keep
    grad_wide = grad_conv.astype(jnp.float32)
    depth_local = jnp.stack(
        [
            jnp.sum(grad_wide * padded[offset : offset + local_frames], axis=0)
            for offset in range(taps)
        ],
        axis=0,
    )
    grad_projected = jnp.concatenate(
        [grad_glu * sigma, grad_glu * linear * sigma * (1.0 - sigma)], axis=1
    ).astype(jnp.bfloat16)
    partial_in = frame_sum(grad_projected, scaled_in).astype(sent)
    rows_in, rows_out = reduce_rows(partial_in, partial_out, span)
    grad_w_in = rows_in * scale
    grad_w_out = rows_out * scale
    columns = grad_projected
    grad_scaled = jnp.dot(
        columns, lax.all_gather(w_in, "ctx", axis=0, tiled=True), preferred_element_type=jnp.float32
    )
    grad_in = norm_backward(grad_scaled * norm_gain, normed_in, inverse_in)
    gains_local = jnp.stack(
        [jnp.sum(grad_scaled * normed_in, axis=0), jnp.sum(grad_gained * normed_conv, axis=0)],
        axis=0,
    )
    blank = jnp.zeros((-(taps + 2) % 16, width), jnp.float32)
    small = jnp.concatenate([depth_local, gains_local, blank], axis=0)
    small = lax.psum_scatter(small.reshape(-1, 128), "ctx", scatter_dimension=0, tiled=True)
    small = lax.all_gather(small, "ctx", axis=0, tiled=True).reshape(-1, width)
    depth_total, gains_total = small[:taps].T, small[taps : taps + 2]
    grad_local = (
        (grad_out.astype(jnp.float32) + grad_in)
        .astype(jnp.bfloat16)
        .reshape(1, local_frames, width)
    )
    grad_frames = lax.all_to_all(grad_local, "ctx", split_axis=1, concat_axis=0, tiled=True)
    return (output, grad_frames, grad_w_in, grad_w_out, depth_total * scale, gains_total * scale)


def solution(mesh):
    placed = (
        P("groups", "ctx", None),
        P(("groups", "ctx"), None),
        P("groups"),
        P(),
        P("ctx", None),
        P(),
        P(),
        P("ctx", None),
    )
    return jax.shard_map(
        shards,
        mesh=mesh,
        in_specs=placed,
        out_specs=(
            P(("groups", "ctx"), None),
            P("groups", "ctx", None),
            P(("groups", "ctx"), None),
            P(("groups", "ctx"), None),
            P("groups", None),
            P("groups", None),
        ),
        check_vma=False,
    )
```

```python
import functools

import jax
import jax.numpy as jnp
from jax import lax
from jax.experimental import pallas as pl
from jax.experimental.pallas import tpu as pltpu
from jax.sharding import PartitionSpec as P

MESH = pl.DeviceIdType.MESH

epsilon = 1e-05


def extended(block, sides, width):
    for axis, dim in sides:
        count = lax.axis_size(axis)
        forward = [(i, i + 1) for i in range(count - 1)]
        backward = [(target, source) for source, target in forward]
        low = lax.ppermute(
            lax.slice_in_dim(block, block.shape[dim] - width, None, axis=dim), axis, forward
        )
        high = lax.ppermute(lax.slice_in_dim(block, 0, width, axis=dim), axis, backward)
        block = jnp.concatenate([low, block, high], axis=dim)
    return block


def normalize(values):
    center = jnp.mean(values, axis=-1, keepdims=True)
    shifted = values - center
    inverse = lax.rsqrt(jnp.mean(shifted * shifted, axis=-1, keepdims=True) + epsilon)
    return (shifted * inverse, inverse)


def norm_backward(upstream, normed, inverse):
    first = jnp.mean(upstream, axis=-1, keepdims=True)
    second = jnp.mean(upstream * normed, axis=-1, keepdims=True)
    return (upstream - first - normed * second) * inverse


def frame_sum(left, right):
    return lax.dot_general(
        left, right, (((0,), (0,)), ((), ())), preferred_element_type=jnp.float32
    )


def times_transposed(left, right):
    return lax.dot_general(
        left, right, (((1,), (1,)), ((), ())), preferred_element_type=jnp.float32
    )


def depthwise(padded, kernel, length):
    total = padded[0:length] * kernel[:, 0]
    for offset in range(1, kernel.shape[1]):
        total = total + padded[offset : offset + length] * kernel[:, offset]
    return total


def depthwise_back(padded, kernel, length):
    taps = kernel.shape[1]
    total = padded[taps - 1 : taps - 1 + length] * kernel[:, 0]
    for offset in range(1, taps):
        begin = taps - 1 - offset
        total = total + padded[begin : begin + length] * kernel[:, offset]
    return total


def grid_of(chips):
    columns = 2 ** ((chips.bit_length() - 1) // 2)
    return (chips // columns, columns)


def chip_at(place, chips):
    rows, columns = grid_of(chips)
    inner = columns - 1
    step = jnp.maximum(place - 1, 0)
    row = lax.div(step, inner)
    column = lax.rem(step, inner)
    column = jnp.where(lax.rem(row, 2) == 0, column, inner - 1 - column)
    snake = row * columns + 1 + column
    back = lax.rem(chips - place, chips) * columns
    return jnp.where((place >= 1) & (place <= rows * inner), snake, back)


def place_of(chip, chips):
    rows, columns = grid_of(chips)
    inner = columns - 1
    row = lax.div(chip, columns)
    column = lax.rem(chip, columns) - 1
    turned = jnp.where(lax.rem(row, 2) == 0, column, inner - 1 - column)
    return jnp.where(column < 0, lax.rem(chips - row, chips), row * inner + turned + 1)


def position(chips):
    me = lax.axis_index("ctx")
    core = lax.rem(me, 2)
    place = place_of(lax.div(me, 2), chips)
    right = chip_at(lax.rem(place + 1, chips), chips) * 2 + core
    left = chip_at(lax.rem(place + chips - 1, chips), chips) * 2 + core
    return (place, core, me + 1 - 2 * core, right, left)


def greet(devices):
    barrier = pltpu.get_barrier_semaphore()
    for device in devices:
        pl.semaphore_signal(barrier, inc=1, device_id={"ctx": device}, device_id_type=MESH)
    pl.semaphore_wait(barrier, len(devices))


def reduce_kernel(
    chips, first_ref, second_ref, first_out, second_out, outgoing, incoming, held, *sems
):
    swap_send, swap_recv, ring_send, ring_recv = sems
    place, core, partner, right, left = position(chips)
    upper = first_ref.shape[2]
    rows = upper + second_ref.shape[2]
    half = first_ref.shape[3] // 2
    parts = ((first_ref, first_out, 0, upper), (second_ref, second_out, upper, rows))
    greet((partner, right, left))

    def owner(way, step):
        ahead = place + 1 + step if way else place + 2 * chips - 1 - step
        return chip_at(lax.rem(ahead, chips), chips)

    def swap(step):
        return pltpu.make_async_remote_copy(
            src_ref=outgoing.at[step],
            dst_ref=incoming.at[step],
            send_sem=swap_send.at[step],
            recv_sem=swap_recv.at[step],
            device_id={"ctx": partner},
            device_id_type=MESH,
        )

    def hop(way, step):
        return pltpu.make_async_remote_copy(
            src_ref=held.at[way, step],
            dst_ref=held.at[way, step + 1],
            send_sem=ring_send.at[way, step],
            recv_sem=ring_recv.at[way, step],
            device_id={"ctx": left if way else right},
            device_id_type=MESH,
        )

    def give(step, carry):
        for way in range(2):
            columns = slice(way * half, (way + 1) * half)
            chip = owner(way, step)
            for source, _, begin, end in parts:
                outgoing[step, begin:end, columns] = source[chip, 1 - core, :, columns]
        swap(step).start()
        return carry

    def total(way, step, part, arrived):
        source, _, begin, end = part
        columns = slice(way * half, (way + 1) * half)
        value = source[owner(way, step), core, :, columns].astype(jnp.float32)
        value = value + incoming[step, begin:end, columns].astype(jnp.float32)
        if arrived:
            value = value + held[way, step, begin:end, :].astype(jnp.float32)
        return value

    def move(step, arrived):
        swap(step).wait_recv()
        for way in range(2):
            if arrived:
                hop(way, step - 1).wait_recv()
            for part in parts:
                held[way, step, part[2] : part[3], :] = total(way, step, part, arrived).astype(
                    held.dtype
                )
            hop(way, step).start()

    lax.fori_loop(0, chips, give, 0)
    move(0, False)

    def middle(step, carry):
        move(step, True)
        return carry

    lax.fori_loop(1, chips - 1, middle, 0)
    swap(chips - 1).wait_recv()
    for way in range(2):
        hop(way, chips - 2).wait_recv()
        for part in parts:
            part[1][:, way * half : (way + 1) * half] = total(way, chips - 1, part, True)

    def drain(step, carry):
        swap(step).wait_send()
        for way in range(2):
            hop(way, step).wait_send()
        return carry

    lax.fori_loop(0, chips - 1, drain, 0)
    swap(chips - 1).wait_send()


def reduce_rows(first, second, span):
    chips = span // 2
    width = first.shape[1]
    upper, lower = first.shape[0] // span, second.shape[0] // span
    rows = upper + lower
    whole = pl.BlockSpec(memory_space=pltpu.VMEM)
    return pl.pallas_call(
        functools.partial(reduce_kernel, chips),
        out_shape=(
            jax.ShapeDtypeStruct((upper, width), jnp.float32),
            jax.ShapeDtypeStruct((lower, width), jnp.float32),
        ),
        in_specs=[whole] * 2,
        out_specs=(whole,) * 2,
        scratch_shapes=[
            pltpu.VMEM((chips, rows, width), first.dtype),
            pltpu.VMEM((chips, rows, width), first.dtype),
            pltpu.VMEM((2, chips, rows, width // 2), first.dtype),
            pltpu.SemaphoreType.DMA((chips,)),
            pltpu.SemaphoreType.DMA((chips,)),
            pltpu.SemaphoreType.DMA((2, chips - 1)),
            pltpu.SemaphoreType.DMA((2, chips - 1)),
        ],
        compiler_params=pltpu.CompilerParams(
            collective_id=0, has_side_effects=True, vmem_limit_bytes=44 * 2**20
        ),
        cost_estimate=pl.CostEstimate(flops=10**7, bytes_accessed=120 * 10**6, transcendentals=0),
        name="reduce_rows",
    )(first.reshape(chips, 2, upper, width), second.reshape(chips, 2, lower, width))


def gather_kernel(
    chips, first_ref, second_ref, first_out, second_out, local, *sems
):
    ring_send, ring_recv, swap_send, swap_recv = sems
    place, core, partner, right, left = position(chips)
    last = chips // 2 - 1
    half = first_ref.shape[1] // 2
    pairs = ((first_ref, first_out), (second_ref, second_out))
    greet((partner, right, left))

    def block(which, way, step, side, cut):
        ahead = place + step if way else place + chips - step
        columns = slice(way * half, (way + 1) * half) if cut else slice(None)
        return pairs[which][1].at[chip_at(lax.rem(ahead, chips), chips), side, :, columns]

    def send(source, target, send_sem, recv_sem, device):
        return pltpu.make_async_remote_copy(
            src_ref=source,
            dst_ref=target,
            send_sem=send_sem,
            recv_sem=recv_sem,
            device_id={"ctx": device},
            device_id_type=MESH,
        )

    def hop(which, way, step, cut, arriving=False, source=None):
        target = block(which, way, step + 1 if arriving else step, core, cut)
        return send(
            target if source is None else source,
            target,
            ring_send.at[which, way, step],
            ring_recv.at[which, way, step],
            left if way else right,
        )

    def swap(which, way, step, side, cut, source=None):
        target = block(which, way, step, side, cut)
        return send(
            target if source is None else source,
            target,
            swap_send.at[which, way, step],
            swap_recv.at[which, way, step],
            partner,
        )

    def keep(which):
        return pltpu.make_async_copy(
            pairs[which][0], block(which, 0, 0, core, False), local.at[which]
        )

    for which in range(2):
        for way in range(2):
            hop(which, way, 0, False, source=pairs[which][0]).start()
    for which in range(2):
        swap(which, 0, 0, core, False, source=pairs[which][0]).start()
        keep(which).start()

    def forward(step, cut):
        for which in range(2):
            for way in range(2):
                hop(which, way, step - 1, False, arriving=True).wait_recv()
                hop(which, way, step, cut).start()
                swap(which, way, step, core, False).start()

    def middle(step, carry):
        forward(step, False)
        return carry

    lax.fori_loop(1, last, middle, 0)
    forward(last, True)
    for which in range(2):
        for way in range(2):
            hop(which, way, last, True, arriving=True).wait_recv()
            swap(which, way, last + 1, core, True).start()

    def drain(step, carry):
        for which in range(2):
            for way in range(2):
                hop(which, way, step, False).wait_send()
                swap(which, way, step + 1, core, False).wait_send()
                swap(which, way, step + 1, 1 - core, False).wait_recv()
        return carry

    lax.fori_loop(0, last, drain, 0)
    for which in range(2):
        keep(which).wait()
        swap(which, 0, 0, core, False, source=pairs[which][0]).wait_send()
        swap(which, 0, 0, 1 - core, False).wait_recv()
        for way in range(2):
            hop(which, way, last, True).wait_send()
            swap(which, way, last + 1, core, True).wait_send()
            swap(which, way, last + 1, 1 - core, True).wait_recv()


def gather_rows(first, second, span):
    chips = span // 2
    width = first.shape[1]
    kept = pl.BlockSpec(memory_space=pl.ANY)
    ring = pltpu.SemaphoreType.DMA((2, 2, chips // 2))
    swaps = pltpu.SemaphoreType.DMA((2, 2, chips // 2 + 1))
    whole_first, whole_second = pl.pallas_call(
        functools.partial(gather_kernel, chips),
        out_shape=(
            jax.ShapeDtypeStruct((chips, 2) + first.shape, first.dtype),
            jax.ShapeDtypeStruct((chips, 2) + second.shape, second.dtype),
        ),
        in_specs=[kept] * 2,
        out_specs=(kept,) * 2,
        scratch_shapes=[pltpu.SemaphoreType.DMA((2,)), ring, ring, swaps, swaps],
        compiler_params=pltpu.CompilerParams(collective_id=1, has_side_effects=True),
        cost_estimate=pl.CostEstimate(flops=10**7, bytes_accessed=120 * 10**6, transcendentals=0),
        name="gather_rows",
    )(first, second)
    return (whole_first.reshape(-1, width), whole_second.reshape(-1, width))


def shards(frames, grad_out, valid_count, norm_gain, w_in, depth_weight, depth_gain, w_out):
    span = lax.axis_size("ctx")
    whole_in, whole_out = gather_rows(w_in, w_out, span)
    ordered = lax.all_to_all(frames, "ctx", split_axis=0, concat_axis=1, tiled=True)
    local_frames = ordered.shape[1]
    width = ordered.shape[2]
    taps = depth_weight.shape[1]
    margin = (taps - 1) // 2
    scale = (local_frames * span) ** (-0.5)
    inputs = ordered.reshape(local_frames, width)
    positions = lax.axis_index("ctx") * local_frames + lax.iota(jnp.int32, local_frames)
    keep = (positions < valid_count[0]).astype(jnp.float32)[:, None]
    wide_in = inputs.astype(jnp.float32)
    normed_in, inverse_in = normalize(wide_in)
    scaled_in = (normed_in * norm_gain).astype(jnp.bfloat16)
    projected = times_transposed(scaled_in, whole_in)
    linear = projected[:, :width]
    sigma = jax.nn.sigmoid(projected[:, width:])
    glu = (linear * sigma * keep).astype(jnp.bfloat16)
    padded = extended(glu, (("ctx", 0),), margin).astype(jnp.float32)
    kernel = depth_weight.astype(jnp.float32)
    conv = depthwise(padded, kernel, local_frames)
    normed_conv, inverse_conv = normalize(conv)
    gained = normed_conv * depth_gain
    sig_two = jax.nn.sigmoid(gained)
    act = (gained * sig_two * keep).astype(jnp.bfloat16)
    mixed = times_transposed(act, whole_out)
    output = (wide_in + mixed).astype(jnp.bfloat16)
    sent = jnp.bfloat16 if span <= 32 else jnp.float32
    partial_out = frame_sum(grad_out, act).astype(sent)
    columns = grad_out
    grad_act = jnp.dot(
        columns,
        whole_out,
        preferred_element_type=jnp.float32,
    )
    grad_gained = grad_act * keep * (sig_two * (1.0 + gained * (1.0 - sig_two)))
    grad_conv = norm_backward(grad_gained * depth_gain, normed_conv, inverse_conv).astype(
        jnp.bfloat16
    )
    grad_pad = extended(grad_conv, (("ctx", 0),), margin).astype(jnp.float32)
    grad_glu = depthwise_back(grad_pad, kernel, local_frames) * keep
    grad_wide = grad_conv.astype(jnp.float32)
    depth_local = jnp.stack(
        [
            jnp.sum(grad_wide * padded[offset : offset + local_frames], axis=0)
            for offset in range(taps)
        ],
        axis=0,
    )
    grad_projected = jnp.concatenate(
        [grad_glu * sigma, grad_glu * linear * sigma * (1.0 - sigma)], axis=1
    ).astype(jnp.bfloat16)
    partial_in = frame_sum(grad_projected, scaled_in).astype(sent)
    rows_in, rows_out = reduce_rows(partial_in, partial_out, span)
    grad_w_in = rows_in * scale
    grad_w_out = rows_out * scale
    columns = grad_projected
    grad_scaled = jnp.dot(
        columns, whole_in, preferred_element_type=jnp.float32
    )
    grad_in = norm_backward(grad_scaled * norm_gain, normed_in, inverse_in)
    gains_local = jnp.stack(
        [jnp.sum(grad_scaled * normed_in, axis=0), jnp.sum(grad_gained * normed_conv, axis=0)],
        axis=0,
    )
    blank = jnp.zeros((-(taps + 2) % 16, width), jnp.float32)
    small = jnp.concatenate([depth_local, gains_local, blank], axis=0)
    small = lax.psum_scatter(small.reshape(-1, 128), "ctx", scatter_dimension=0, tiled=True)
    small = lax.all_gather(small, "ctx", axis=0, tiled=True).reshape(-1, width)
    depth_total, gains_total = small[:taps].T, small[taps : taps + 2]
    grad_local = (grad_out.astype(jnp.float32) + grad_in).astype(jnp.bfloat16)
    grad_frames = lax.all_to_all(
        grad_local.reshape(frames.shape), "ctx", split_axis=0, concat_axis=0, tiled=True
    )
    return (output, grad_frames, grad_w_in, grad_w_out, depth_total * scale, gains_total * scale)


def solution(mesh):
    placed = (
        P("groups", "ctx", None),
        P(("groups", "ctx"), None),
        P("groups"),
        P(),
        P("ctx", None),
        P(),
        P(),
        P("ctx", None),
    )
    return jax.shard_map(
        shards,
        mesh=mesh,
        in_specs=placed,
        out_specs=(
            P(("groups", "ctx"), None),
            P("groups", "ctx", None),
            P(("groups", "ctx"), None),
            P(("groups", "ctx"), None),
            P("groups", None),
            P("groups", None),
        ),
        check_vma=False,
    )
```

```python
import functools

import jax
import jax.numpy as jnp
from jax import lax
from jax.experimental import pallas as pl
from jax.experimental.pallas import tpu as pltpu
from jax.sharding import PartitionSpec as P

MESH = pl.DeviceIdType.MESH

epsilon = 1e-05


def extended(block, sides, width):
    for axis, dim in sides:
        count = lax.axis_size(axis)
        forward = [(i, i + 1) for i in range(count - 1)]
        backward = [(target, source) for source, target in forward]
        low = lax.ppermute(
            lax.slice_in_dim(block, block.shape[dim] - width, None, axis=dim), axis, forward
        )
        high = lax.ppermute(lax.slice_in_dim(block, 0, width, axis=dim), axis, backward)
        block = jnp.concatenate([low, block, high], axis=dim)
    return block


def normalize(values):
    center = jnp.mean(values, axis=-1, keepdims=True)
    shifted = values - center
    inverse = lax.rsqrt(jnp.mean(shifted * shifted, axis=-1, keepdims=True) + epsilon)
    return (shifted * inverse, inverse)


def norm_backward(upstream, normed, inverse):
    first = jnp.mean(upstream, axis=-1, keepdims=True)
    second = jnp.mean(upstream * normed, axis=-1, keepdims=True)
    return (upstream - first - normed * second) * inverse


def frame_sum(left, right):
    return lax.dot_general(
        left, right, (((0,), (0,)), ((), ())), preferred_element_type=jnp.float32
    )


def times_transposed(left, right):
    return lax.dot_general(
        left, right, (((1,), (1,)), ((), ())), preferred_element_type=jnp.float32
    )


def depthwise(padded, kernel, length):
    total = padded[0:length] * kernel[:, 0]
    for offset in range(1, kernel.shape[1]):
        total = total + padded[offset : offset + length] * kernel[:, offset]
    return total


def depthwise_back(padded, kernel, length):
    taps = kernel.shape[1]
    total = padded[taps - 1 : taps - 1 + length] * kernel[:, 0]
    for offset in range(1, taps):
        begin = taps - 1 - offset
        total = total + padded[begin : begin + length] * kernel[:, offset]
    return total


def grid_of(chips):
    columns = 2 ** ((chips.bit_length() - 1) // 2)
    return (chips // columns, columns)


def chip_at(place, chips):
    rows, columns = grid_of(chips)
    inner = columns - 1
    step = jnp.maximum(place - 1, 0)
    row = lax.div(step, inner)
    column = lax.rem(step, inner)
    column = jnp.where(lax.rem(row, 2) == 0, column, inner - 1 - column)
    snake = row * columns + 1 + column
    back = lax.rem(chips - place, chips) * columns
    return jnp.where((place >= 1) & (place <= rows * inner), snake, back)


def place_of(chip, chips):
    rows, columns = grid_of(chips)
    inner = columns - 1
    row = lax.div(chip, columns)
    column = lax.rem(chip, columns) - 1
    turned = jnp.where(lax.rem(row, 2) == 0, column, inner - 1 - column)
    return jnp.where(column < 0, lax.rem(chips - row, chips), row * inner + turned + 1)


def position(chips):
    me = lax.axis_index("ctx")
    core = lax.rem(me, 2)
    place = place_of(lax.div(me, 2), chips)
    right = chip_at(lax.rem(place + 1, chips), chips) * 2 + core
    left = chip_at(lax.rem(place + chips - 1, chips), chips) * 2 + core
    return (place, core, me + 1 - 2 * core, right, left)


def greet(devices):
    barrier = pltpu.get_barrier_semaphore()
    for device in devices:
        pl.semaphore_signal(barrier, inc=1, device_id={"ctx": device}, device_id_type=MESH)
    pl.semaphore_wait(barrier, len(devices))


def reduce_kernel(
    chips,
    first_ref,
    second_ref,
    small_ref,
    first_out,
    second_out,
    small_out,
    outgoing,
    incoming,
    held,
    pieces,
    theirs,
    slots,
    totals,
    *sems,
):
    swap_send, swap_recv, ring_send, ring_recv = sems[:4]
    piece_send, piece_recv, slot_send, slot_recv = sems[4:]
    place, core, partner, right, left = position(chips)
    upper = first_ref.shape[2]
    rows = upper + second_ref.shape[2]
    half = first_ref.shape[3] // 2
    parts = ((first_ref, first_out, 0, upper), (second_ref, second_out, upper, rows))
    greet((partner, right, left))

    def owner(way, step):
        ahead = place + 1 + step if way else place + 2 * chips - 1 - step
        return chip_at(lax.rem(ahead, chips), chips)

    def swap(step):
        return pltpu.make_async_remote_copy(
            src_ref=outgoing.at[step],
            dst_ref=incoming.at[step],
            send_sem=swap_send.at[step],
            recv_sem=swap_recv.at[step],
            device_id={"ctx": partner},
            device_id_type=MESH,
        )

    def hop(way, step):
        return pltpu.make_async_remote_copy(
            src_ref=held.at[way, step],
            dst_ref=held.at[way, step + 1],
            send_sem=ring_send.at[way, step],
            recv_sem=ring_recv.at[way, step],
            device_id={"ctx": left if way else right},
            device_id_type=MESH,
        )

    def exchange(source, target, index):
        return pltpu.make_async_remote_copy(
            src_ref=source,
            dst_ref=target,
            send_sem=piece_send.at[index],
            recv_sem=piece_recv.at[index],
            device_id={"ctx": partner},
            device_id_type=MESH,
        )

    def relay(way, step, arriving=False):
        distance = step + 1 if arriving else step
        ahead = place + distance if way else place + chips - distance
        slot = slots.at[chip_at(lax.rem(ahead, chips), chips)]
        return pltpu.make_async_remote_copy(
            src_ref=slot,
            dst_ref=slot,
            send_sem=slot_send.at[way, step],
            recv_sem=slot_recv.at[way, step],
            device_id={"ctx": left if way else right},
            device_id_type=MESH,
        )

    for side in range(2):
        pieces[side] = small_ref[:, side * half : (side + 1) * half]
    exchange(pieces.at[1 - core], theirs, 0).start()

    def give(step, carry):
        for way in range(2):
            columns = slice(way * half, (way + 1) * half)
            chip = owner(way, step)
            for source, _, begin, end in parts:
                outgoing[step, begin:end, columns] = source[chip, 1 - core, :, columns]
        swap(step).start()
        return carry

    def total(way, step, part, arrived):
        source, _, begin, end = part
        columns = slice(way * half, (way + 1) * half)
        value = source[owner(way, step), core, :, columns].astype(jnp.float32)
        value = value + incoming[step, begin:end, columns].astype(jnp.float32)
        if arrived:
            value = value + held[way, step, begin:end, :].astype(jnp.float32)
        return value

    def move(step, arrived):
        swap(step).wait_recv()
        for way in range(2):
            if arrived:
                hop(way, step - 1).wait_recv()
            for part in parts:
                held[way, step, part[2] : part[3], :] = total(way, step, part, arrived).astype(
                    held.dtype
                )
            hop(way, step).start()

    lax.fori_loop(0, chips, give, 0)
    exchange(pieces.at[1 - core], theirs, 0).wait_recv()
    slots[chip_at(place, chips)] = (pieces[core] + theirs[...]).astype(slots.dtype)
    move(0, False)
    for way in range(2):
        relay(way, 0).start()
    turn = chips // 2

    def early(step, carry):
        move(step, True)
        for way in range(2):
            relay(way, step - 1, True).wait_recv()
            relay(way, step).start()
        return carry

    lax.fori_loop(1, turn - 1, early, 0)
    move(turn - 1, True)
    for way in range(2):
        relay(way, turn - 2, True).wait_recv()
    relay(0, turn - 1).start()
    move(turn, True)
    relay(0, turn - 1, True).wait_recv()

    def add(chip, value):
        return value + slots[chip].astype(jnp.float32)

    totals[core] = lax.fori_loop(1, chips, add, slots[0].astype(jnp.float32))
    exchange(totals.at[core], totals.at[core], 1).start()

    def middle(step, carry):
        move(step, True)
        return carry

    lax.fori_loop(turn + 1, chips - 1, middle, 0)
    swap(chips - 1).wait_recv()
    for way in range(2):
        hop(way, chips - 2).wait_recv()
        for part in parts:
            part[1][:, way * half : (way + 1) * half] = total(way, chips - 1, part, True)

    def drain(step, carry):
        swap(step).wait_send()
        for way in range(2):
            hop(way, step).wait_send()
        return carry

    lax.fori_loop(0, chips - 1, drain, 0)
    swap(chips - 1).wait_send()
    exchange(totals.at[1 - core], totals.at[1 - core], 1).wait_recv()
    for side in range(2):
        small_out[:, side * half : (side + 1) * half] = totals[side]
    exchange(pieces.at[1 - core], theirs, 0).wait_send()
    exchange(totals.at[core], totals.at[core], 1).wait_send()

    def settle(step, carry):
        for way in range(2):
            relay(way, step).wait_send()
        return carry

    lax.fori_loop(0, turn - 1, settle, 0)
    relay(0, turn - 1).wait_send()


def reduce_rows(first, second, small, span):
    chips = span // 2
    width = first.shape[1]
    upper, lower = first.shape[0] // span, second.shape[0] // span
    rows = upper + lower
    whole = pl.BlockSpec(memory_space=pltpu.VMEM)
    return pl.pallas_call(
        functools.partial(reduce_kernel, chips),
        out_shape=(
            jax.ShapeDtypeStruct((upper, width), jnp.float32),
            jax.ShapeDtypeStruct((lower, width), jnp.float32),
            jax.ShapeDtypeStruct(small.shape, jnp.float32),
        ),
        in_specs=[whole] * 3,
        out_specs=(whole,) * 3,
        scratch_shapes=[
            pltpu.VMEM((chips, rows, width), first.dtype),
            pltpu.VMEM((chips, rows, width), first.dtype),
            pltpu.VMEM((2, chips, rows, width // 2), first.dtype),
            pltpu.VMEM((2, small.shape[0], width // 2), jnp.float32),
            pltpu.VMEM((small.shape[0], width // 2), jnp.float32),
            pltpu.VMEM((chips, small.shape[0], width // 2), first.dtype),
            pltpu.VMEM((2, small.shape[0], width // 2), jnp.float32),
            pltpu.SemaphoreType.DMA((chips,)),
            pltpu.SemaphoreType.DMA((chips,)),
            pltpu.SemaphoreType.DMA((2, chips - 1)),
            pltpu.SemaphoreType.DMA((2, chips - 1)),
            pltpu.SemaphoreType.DMA((2,)),
            pltpu.SemaphoreType.DMA((2,)),
            pltpu.SemaphoreType.DMA((2, chips // 2)),
            pltpu.SemaphoreType.DMA((2, chips // 2)),
        ],
        compiler_params=pltpu.CompilerParams(
            collective_id=0, has_side_effects=True, vmem_limit_bytes=44 * 2**20
        ),
        cost_estimate=pl.CostEstimate(flops=10**7, bytes_accessed=120 * 10**6, transcendentals=0),
        name="reduce_rows",
    )(first.reshape(chips, 2, upper, width), second.reshape(chips, 2, lower, width), small)


def gather_kernel(
    chips, first_ref, second_ref, first_out, second_out, local, *sems
):
    ring_send, ring_recv, swap_send, swap_recv = sems
    place, core, partner, right, left = position(chips)
    last = chips // 2 - 1
    half = first_ref.shape[1] // 2
    pairs = ((first_ref, first_out), (second_ref, second_out))
    greet((partner, right, left))

    def block(which, way, step, side, cut):
        ahead = place + step if way else place + chips - step
        columns = slice(way * half, (way + 1) * half) if cut else slice(None)
        return pairs[which][1].at[chip_at(lax.rem(ahead, chips), chips), side, :, columns]

    def send(source, target, send_sem, recv_sem, device):
        return pltpu.make_async_remote_copy(
            src_ref=source,
            dst_ref=target,
            send_sem=send_sem,
            recv_sem=recv_sem,
            device_id={"ctx": device},
            device_id_type=MESH,
        )

    def hop(which, way, step, cut, arriving=False, source=None):
        target = block(which, way, step + 1 if arriving else step, core, cut)
        return send(
            target if source is None else source,
            target,
            ring_send.at[which, way, step],
            ring_recv.at[which, way, step],
            left if way else right,
        )

    def swap(which, way, step, side, cut, source=None):
        target = block(which, way, step, side, cut)
        return send(
            target if source is None else source,
            target,
            swap_send.at[which, way, step],
            swap_recv.at[which, way, step],
            partner,
        )

    def keep(which):
        return pltpu.make_async_copy(
            pairs[which][0], block(which, 0, 0, core, False), local.at[which]
        )

    for which in range(2):
        for way in range(2):
            hop(which, way, 0, False, source=pairs[which][0]).start()
    for which in range(2):
        swap(which, 0, 0, core, False, source=pairs[which][0]).start()
        keep(which).start()

    def forward(step, cut):
        for which in range(2):
            for way in range(2):
                hop(which, way, step - 1, False, arriving=True).wait_recv()
                hop(which, way, step, cut).start()
                swap(which, way, step, core, False).start()

    def middle(step, carry):
        forward(step, False)
        return carry

    lax.fori_loop(1, last, middle, 0)
    forward(last, True)
    for which in range(2):
        for way in range(2):
            hop(which, way, last, True, arriving=True).wait_recv()
            swap(which, way, last + 1, core, True).start()

    def drain(step, carry):
        for which in range(2):
            for way in range(2):
                hop(which, way, step, False).wait_send()
                swap(which, way, step + 1, core, False).wait_send()
                swap(which, way, step + 1, 1 - core, False).wait_recv()
        return carry

    lax.fori_loop(0, last, drain, 0)
    for which in range(2):
        keep(which).wait()
        swap(which, 0, 0, core, False, source=pairs[which][0]).wait_send()
        swap(which, 0, 0, 1 - core, False).wait_recv()
        for way in range(2):
            hop(which, way, last, True).wait_send()
            swap(which, way, last + 1, core, True).wait_send()
            swap(which, way, last + 1, 1 - core, True).wait_recv()


def gather_rows(first, second, span):
    chips = span // 2
    width = first.shape[1]
    kept = pl.BlockSpec(memory_space=pl.ANY)
    ring = pltpu.SemaphoreType.DMA((2, 2, chips // 2))
    swaps = pltpu.SemaphoreType.DMA((2, 2, chips // 2 + 1))
    whole_first, whole_second = pl.pallas_call(
        functools.partial(gather_kernel, chips),
        out_shape=(
            jax.ShapeDtypeStruct((chips, 2) + first.shape, first.dtype),
            jax.ShapeDtypeStruct((chips, 2) + second.shape, second.dtype),
        ),
        in_specs=[kept] * 2,
        out_specs=(kept,) * 2,
        scratch_shapes=[pltpu.SemaphoreType.DMA((2,)), ring, ring, swaps, swaps],
        compiler_params=pltpu.CompilerParams(collective_id=1, has_side_effects=True),
        cost_estimate=pl.CostEstimate(flops=10**7, bytes_accessed=120 * 10**6, transcendentals=0),
        name="gather_rows",
    )(first, second)
    return (whole_first.reshape(-1, width), whole_second.reshape(-1, width))


def shards(frames, grad_out, valid_count, norm_gain, w_in, depth_weight, depth_gain, w_out):
    span = lax.axis_size("ctx")
    whole_in, whole_out = gather_rows(w_in, w_out, span)
    ordered = lax.all_to_all(frames, "ctx", split_axis=0, concat_axis=1, tiled=True)
    local_frames = ordered.shape[1]
    width = ordered.shape[2]
    taps = depth_weight.shape[1]
    margin = (taps - 1) // 2
    scale = (local_frames * span) ** (-0.5)
    inputs = ordered.reshape(local_frames, width)
    positions = lax.axis_index("ctx") * local_frames + lax.iota(jnp.int32, local_frames)
    keep = (positions < valid_count[0]).astype(jnp.float32)[:, None]
    wide_in = inputs.astype(jnp.float32)
    normed_in, inverse_in = normalize(wide_in)
    scaled_in = (normed_in * norm_gain).astype(jnp.bfloat16)
    projected = times_transposed(scaled_in, whole_in)
    linear = projected[:, :width]
    sigma = jax.nn.sigmoid(projected[:, width:])
    glu = (linear * sigma * keep).astype(jnp.bfloat16)
    padded = extended(glu, (("ctx", 0),), margin).astype(jnp.float32)
    kernel = depth_weight.astype(jnp.float32)
    conv = depthwise(padded, kernel, local_frames)
    normed_conv, inverse_conv = normalize(conv)
    gained = normed_conv * depth_gain
    sig_two = jax.nn.sigmoid(gained)
    act = (gained * sig_two * keep).astype(jnp.bfloat16)
    mixed = times_transposed(act, whole_out)
    output = (wide_in + mixed).astype(jnp.bfloat16)
    sent = jnp.bfloat16 if span <= 32 else jnp.float32
    partial_out = frame_sum(grad_out, act).astype(sent)
    columns = grad_out
    grad_act = jnp.dot(
        columns,
        whole_out,
        preferred_element_type=jnp.float32,
    )
    grad_gained = grad_act * keep * (sig_two * (1.0 + gained * (1.0 - sig_two)))
    grad_conv = norm_backward(grad_gained * depth_gain, normed_conv, inverse_conv).astype(
        jnp.bfloat16
    )
    grad_pad = extended(grad_conv, (("ctx", 0),), margin).astype(jnp.float32)
    grad_glu = depthwise_back(grad_pad, kernel, local_frames) * keep
    grad_wide = grad_conv.astype(jnp.float32)
    depth_local = jnp.stack(
        [
            jnp.sum(grad_wide * padded[offset : offset + local_frames], axis=0)
            for offset in range(taps)
        ],
        axis=0,
    )
    grad_projected = jnp.concatenate(
        [grad_glu * sigma, grad_glu * linear * sigma * (1.0 - sigma)], axis=1
    ).astype(jnp.bfloat16)
    partial_in = frame_sum(grad_projected, scaled_in).astype(sent)
    columns = grad_projected
    grad_scaled = jnp.dot(
        columns, whole_in, preferred_element_type=jnp.float32
    )
    grad_in = norm_backward(grad_scaled * norm_gain, normed_in, inverse_in)
    gains_local = jnp.stack(
        [jnp.sum(grad_scaled * normed_in, axis=0), jnp.sum(grad_gained * normed_conv, axis=0)],
        axis=0,
    )
    blank = jnp.zeros((-(taps + 2) % 16, width), jnp.float32)
    small = jnp.concatenate([depth_local, gains_local, blank], axis=0)
    rows_in, rows_out, small = reduce_rows(partial_in, partial_out, small, span)
    grad_w_in = rows_in * scale
    grad_w_out = rows_out * scale
    depth_total, gains_total = small[:taps].T, small[taps : taps + 2]
    grad_local = (grad_out.astype(jnp.float32) + grad_in).astype(jnp.bfloat16)
    grad_frames = lax.all_to_all(
        grad_local.reshape(frames.shape), "ctx", split_axis=0, concat_axis=0, tiled=True
    )
    return (output, grad_frames, grad_w_in, grad_w_out, depth_total * scale, gains_total * scale)


def solution(mesh):
    placed = (
        P("groups", "ctx", None),
        P(("groups", "ctx"), None),
        P("groups"),
        P(),
        P("ctx", None),
        P(),
        P(),
        P("ctx", None),
    )
    return jax.shard_map(
        shards,
        mesh=mesh,
        in_specs=placed,
        out_specs=(
            P(("groups", "ctx"), None),
            P("groups", "ctx", None),
            P(("groups", "ctx"), None),
            P(("groups", "ctx"), None),
            P("groups", None),
            P("groups", None),
        ),
        check_vma=False,
    )
```

```python
import functools

import jax
import jax.numpy as jnp
from jax import lax
from jax.experimental import pallas as pl
from jax.experimental.pallas import tpu as pltpu
from jax.sharding import PartitionSpec as P

MESH = pl.DeviceIdType.MESH

epsilon = 1e-05


def extended(block, sides, width):
    for axis, dim in sides:
        count = lax.axis_size(axis)
        forward = [(i, i + 1) for i in range(count - 1)]
        backward = [(target, source) for source, target in forward]
        low = lax.ppermute(
            lax.slice_in_dim(block, block.shape[dim] - width, None, axis=dim), axis, forward
        )
        high = lax.ppermute(lax.slice_in_dim(block, 0, width, axis=dim), axis, backward)
        block = jnp.concatenate([low, block, high], axis=dim)
    return block


def normalize(values):
    center = jnp.mean(values, axis=-1, keepdims=True)
    shifted = values - center
    inverse = lax.rsqrt(jnp.mean(shifted * shifted, axis=-1, keepdims=True) + epsilon)
    return (shifted * inverse, inverse)


def norm_backward(upstream, normed, inverse):
    first = jnp.mean(upstream, axis=-1, keepdims=True)
    second = jnp.mean(upstream * normed, axis=-1, keepdims=True)
    return (upstream - first - normed * second) * inverse


def frame_sum(left, right):
    return lax.dot_general(
        left, right, (((0,), (0,)), ((), ())), preferred_element_type=jnp.float32
    )


def times_transposed(left, right):
    return lax.dot_general(
        left, right, (((1,), (1,)), ((), ())), preferred_element_type=jnp.float32
    )


def depthwise(padded, kernel, length):
    total = padded[0:length] * kernel[:, 0]
    for offset in range(1, kernel.shape[1]):
        total = total + padded[offset : offset + length] * kernel[:, offset]
    return total


def depthwise_back(padded, kernel, length):
    taps = kernel.shape[1]
    total = padded[taps - 1 : taps - 1 + length] * kernel[:, 0]
    for offset in range(1, taps):
        begin = taps - 1 - offset
        total = total + padded[begin : begin + length] * kernel[:, offset]
    return total


def grid_of(chips):
    columns = 2 ** ((chips.bit_length() - 1) // 2)
    return (chips // columns, columns)


def chip_at(place, chips):
    rows, columns = grid_of(chips)
    inner = columns - 1
    step = jnp.maximum(place - 1, 0)
    row = lax.div(step, inner)
    column = lax.rem(step, inner)
    column = jnp.where(lax.rem(row, 2) == 0, column, inner - 1 - column)
    snake = row * columns + 1 + column
    back = lax.rem(chips - place, chips) * columns
    return jnp.where((place >= 1) & (place <= rows * inner), snake, back)


def place_of(chip, chips):
    rows, columns = grid_of(chips)
    inner = columns - 1
    row = lax.div(chip, columns)
    column = lax.rem(chip, columns) - 1
    turned = jnp.where(lax.rem(row, 2) == 0, column, inner - 1 - column)
    return jnp.where(column < 0, lax.rem(chips - row, chips), row * inner + turned + 1)


def position(chips):
    me = lax.axis_index("ctx")
    core = lax.rem(me, 2)
    place = place_of(lax.div(me, 2), chips)
    right = chip_at(lax.rem(place + 1, chips), chips) * 2 + core
    left = chip_at(lax.rem(place + chips - 1, chips), chips) * 2 + core
    return (place, core, me + 1 - 2 * core, right, left)


def greet(devices):
    barrier = pltpu.get_barrier_semaphore()
    for device in devices:
        pl.semaphore_signal(barrier, inc=1, device_id={"ctx": device}, device_id_type=MESH)
    pl.semaphore_wait(barrier, len(devices))


def reduce_kernel(
    chips,
    first_ref,
    small_ref,
    first_out,
    small_out,
    outgoing,
    incoming,
    held,
    pieces,
    theirs,
    slots,
    totals,
    *sems,
):
    swap_send, swap_recv, ring_send, ring_recv = sems[:4]
    piece_send, piece_recv, slot_send, slot_recv = sems[4:]
    place, core, partner, right, left = position(chips)
    half = first_ref.shape[3] // 2
    parts = ((first_ref, first_out, 0, first_ref.shape[2]),)
    greet((partner, right, left))

    def owner(way, step):
        ahead = place + 1 + step if way else place + 2 * chips - 1 - step
        return chip_at(lax.rem(ahead, chips), chips)

    def swap(step):
        return pltpu.make_async_remote_copy(
            src_ref=outgoing.at[step],
            dst_ref=incoming.at[step],
            send_sem=swap_send.at[step],
            recv_sem=swap_recv.at[step],
            device_id={"ctx": partner},
            device_id_type=MESH,
        )

    def hop(way, step):
        return pltpu.make_async_remote_copy(
            src_ref=held.at[way, step],
            dst_ref=held.at[way, step + 1],
            send_sem=ring_send.at[way, step],
            recv_sem=ring_recv.at[way, step],
            device_id={"ctx": left if way else right},
            device_id_type=MESH,
        )

    def exchange(source, target, index):
        return pltpu.make_async_remote_copy(
            src_ref=source,
            dst_ref=target,
            send_sem=piece_send.at[index],
            recv_sem=piece_recv.at[index],
            device_id={"ctx": partner},
            device_id_type=MESH,
        )

    def relay(way, step, arriving=False):
        distance = step + 1 if arriving else step
        ahead = place + distance if way else place + chips - distance
        slot = slots.at[chip_at(lax.rem(ahead, chips), chips)]
        return pltpu.make_async_remote_copy(
            src_ref=slot,
            dst_ref=slot,
            send_sem=slot_send.at[way, step],
            recv_sem=slot_recv.at[way, step],
            device_id={"ctx": left if way else right},
            device_id_type=MESH,
        )

    for side in range(2):
        pieces[side] = small_ref[:, side * half : (side + 1) * half]
    exchange(pieces.at[1 - core], theirs, 0).start()

    def give(step, carry):
        for way in range(2):
            columns = slice(way * half, (way + 1) * half)
            chip = owner(way, step)
            for source, _, begin, end in parts:
                outgoing[step, begin:end, columns] = source[chip, 1 - core, :, columns]
        swap(step).start()
        return carry

    def total(way, step, part, arrived):
        source, _, begin, end = part
        columns = slice(way * half, (way + 1) * half)
        value = source[owner(way, step), core, :, columns].astype(jnp.float32)
        value = value + incoming[step, begin:end, columns].astype(jnp.float32)
        if arrived:
            value = value + held[way, step, begin:end, :].astype(jnp.float32)
        return value

    def move(step, arrived):
        swap(step).wait_recv()
        for way in range(2):
            if arrived:
                hop(way, step - 1).wait_recv()
            for part in parts:
                held[way, step, part[2] : part[3], :] = total(way, step, part, arrived).astype(
                    held.dtype
                )
            hop(way, step).start()

    lax.fori_loop(0, chips, give, 0)
    exchange(pieces.at[1 - core], theirs, 0).wait_recv()
    slots[chip_at(place, chips)] = (pieces[core] + theirs[...]).astype(slots.dtype)
    move(0, False)
    for way in range(2):
        relay(way, 0).start()
    turn = chips // 2

    def early(step, carry):
        move(step, True)
        for way in range(2):
            relay(way, step - 1, True).wait_recv()
            relay(way, step).start()
        return carry

    lax.fori_loop(1, turn - 1, early, 0)
    move(turn - 1, True)
    for way in range(2):
        relay(way, turn - 2, True).wait_recv()
    relay(0, turn - 1).start()
    move(turn, True)
    relay(0, turn - 1, True).wait_recv()

    def add(chip, value):
        return value + slots[chip].astype(jnp.float32)

    totals[core] = lax.fori_loop(1, chips, add, slots[0].astype(jnp.float32))
    exchange(totals.at[core], totals.at[core], 1).start()

    def middle(step, carry):
        move(step, True)
        return carry

    lax.fori_loop(turn + 1, chips - 1, middle, 0)
    swap(chips - 1).wait_recv()
    for way in range(2):
        hop(way, chips - 2).wait_recv()
        for part in parts:
            part[1][:, way * half : (way + 1) * half] = total(way, chips - 1, part, True)

    def drain(step, carry):
        swap(step).wait_send()
        for way in range(2):
            hop(way, step).wait_send()
        return carry

    lax.fori_loop(0, chips - 1, drain, 0)
    swap(chips - 1).wait_send()
    exchange(totals.at[1 - core], totals.at[1 - core], 1).wait_recv()
    for side in range(2):
        small_out[:, side * half : (side + 1) * half] = totals[side]
    exchange(pieces.at[1 - core], theirs, 0).wait_send()
    exchange(totals.at[core], totals.at[core], 1).wait_send()

    def settle(step, carry):
        for way in range(2):
            relay(way, step).wait_send()
        return carry

    lax.fori_loop(0, turn - 1, settle, 0)
    relay(0, turn - 1).wait_send()


def reduce_rows(first, small, span):
    chips = span // 2
    width = first.shape[1]
    rows = first.shape[0] // span
    whole = pl.BlockSpec(memory_space=pltpu.VMEM)
    return pl.pallas_call(
        functools.partial(reduce_kernel, chips),
        out_shape=(
            jax.ShapeDtypeStruct((rows, width), jnp.float32),
            jax.ShapeDtypeStruct(small.shape, jnp.float32),
        ),
        in_specs=[whole] * 2,
        out_specs=(whole,) * 2,
        scratch_shapes=[
            pltpu.VMEM((chips, rows, width), first.dtype),
            pltpu.VMEM((chips, rows, width), first.dtype),
            pltpu.VMEM((2, chips, rows, width // 2), first.dtype),
            pltpu.VMEM((2, small.shape[0], width // 2), jnp.float32),
            pltpu.VMEM((small.shape[0], width // 2), jnp.float32),
            pltpu.VMEM((chips, small.shape[0], width // 2), first.dtype),
            pltpu.VMEM((2, small.shape[0], width // 2), jnp.float32),
            pltpu.SemaphoreType.DMA((chips,)),
            pltpu.SemaphoreType.DMA((chips,)),
            pltpu.SemaphoreType.DMA((2, chips - 1)),
            pltpu.SemaphoreType.DMA((2, chips - 1)),
            pltpu.SemaphoreType.DMA((2,)),
            pltpu.SemaphoreType.DMA((2,)),
            pltpu.SemaphoreType.DMA((2, chips // 2)),
            pltpu.SemaphoreType.DMA((2, chips // 2)),
        ],
        compiler_params=pltpu.CompilerParams(
            collective_id=0, has_side_effects=True, vmem_limit_bytes=44 * 2**20
        ),
        cost_estimate=pl.CostEstimate(flops=10**7, bytes_accessed=120 * 10**6, transcendentals=0),
        name="reduce_rows",
    )(first.reshape(chips, 2, rows, width), small)


def gather_kernel(
    chips, first_ref, first_out, local, *sems
):
    ring_send, ring_recv, swap_send, swap_recv = sems
    place, core, partner, right, left = position(chips)
    last = chips // 2 - 1
    half = first_ref.shape[1] // 2
    pairs = ((first_ref, first_out),)
    greet((partner, right, left))

    def block(which, way, step, side, cut):
        ahead = place + step if way else place + chips - step
        columns = slice(way * half, (way + 1) * half) if cut else slice(None)
        return pairs[which][1].at[chip_at(lax.rem(ahead, chips), chips), side, :, columns]

    def send(source, target, send_sem, recv_sem, device):
        return pltpu.make_async_remote_copy(
            src_ref=source,
            dst_ref=target,
            send_sem=send_sem,
            recv_sem=recv_sem,
            device_id={"ctx": device},
            device_id_type=MESH,
        )

    def hop(which, way, step, cut, arriving=False, source=None):
        target = block(which, way, step + 1 if arriving else step, core, cut)
        return send(
            target if source is None else source,
            target,
            ring_send.at[which, way, step],
            ring_recv.at[which, way, step],
            left if way else right,
        )

    def swap(which, way, step, side, cut, source=None):
        target = block(which, way, step, side, cut)
        return send(
            target if source is None else source,
            target,
            swap_send.at[which, way, step],
            swap_recv.at[which, way, step],
            partner,
        )

    def keep(which):
        return pltpu.make_async_copy(
            pairs[which][0], block(which, 0, 0, core, False), local.at[which]
        )

    for which in range(1):
        for way in range(2):
            hop(which, way, 0, False, source=pairs[which][0]).start()
    for which in range(1):
        swap(which, 0, 0, core, False, source=pairs[which][0]).start()
        keep(which).start()

    def forward(step, cut):
        for which in range(1):
            for way in range(2):
                hop(which, way, step - 1, False, arriving=True).wait_recv()
                hop(which, way, step, cut).start()
                swap(which, way, step, core, False).start()

    def middle(step, carry):
        forward(step, False)
        return carry

    lax.fori_loop(1, last, middle, 0)
    forward(last, True)
    for which in range(1):
        for way in range(2):
            hop(which, way, last, True, arriving=True).wait_recv()
            swap(which, way, last + 1, core, True).start()

    def drain(step, carry):
        for which in range(1):
            for way in range(2):
                hop(which, way, step, False).wait_send()
                swap(which, way, step + 1, core, False).wait_send()
                swap(which, way, step + 1, 1 - core, False).wait_recv()
        return carry

    lax.fori_loop(0, last, drain, 0)
    for which in range(1):
        keep(which).wait()
        swap(which, 0, 0, core, False, source=pairs[which][0]).wait_send()
        swap(which, 0, 0, 1 - core, False).wait_recv()
        for way in range(2):
            hop(which, way, last, True).wait_send()
            swap(which, way, last + 1, core, True).wait_send()
            swap(which, way, last + 1, 1 - core, True).wait_recv()


def gather_rows(first, span):
    chips = span // 2
    width = first.shape[1]
    kept = pl.BlockSpec(memory_space=pl.ANY)
    ring = pltpu.SemaphoreType.DMA((1, 2, chips // 2))
    swaps = pltpu.SemaphoreType.DMA((1, 2, chips // 2 + 1))
    whole = pl.pallas_call(
        functools.partial(gather_kernel, chips),
        out_shape=jax.ShapeDtypeStruct((chips, 2) + first.shape, first.dtype),
        in_specs=[kept],
        out_specs=kept,
        scratch_shapes=[pltpu.SemaphoreType.DMA((1,)), ring, ring, swaps, swaps],
        compiler_params=pltpu.CompilerParams(collective_id=1, has_side_effects=True),
        cost_estimate=pl.CostEstimate(flops=10**7, bytes_accessed=120 * 10**6, transcendentals=0),
        name="gather_rows",
    )(first)
    return whole.reshape(-1, width)


def shards(frames, grad_out, valid_count, norm_gain, w_in, depth_weight, depth_gain, w_out):
    span = lax.axis_size("ctx")
    whole_in = gather_rows(w_in, span)
    whole_out = lax.all_gather(w_out, "ctx", axis=0, tiled=True)
    ordered = lax.all_to_all(frames, "ctx", split_axis=0, concat_axis=1, tiled=True)
    local_frames = ordered.shape[1]
    width = ordered.shape[2]
    taps = depth_weight.shape[1]
    margin = (taps - 1) // 2
    scale = (local_frames * span) ** (-0.5)
    inputs = ordered.reshape(local_frames, width)
    positions = lax.axis_index("ctx") * local_frames + lax.iota(jnp.int32, local_frames)
    keep = (positions < valid_count[0]).astype(jnp.float32)[:, None]
    wide_in = inputs.astype(jnp.float32)
    normed_in, inverse_in = normalize(wide_in)
    scaled_in = (normed_in * norm_gain).astype(jnp.bfloat16)
    projected = times_transposed(scaled_in, whole_in)
    linear = projected[:, :width]
    sigma = jax.nn.sigmoid(projected[:, width:])
    glu = (linear * sigma * keep).astype(jnp.bfloat16)
    padded = extended(glu, (("ctx", 0),), margin).astype(jnp.float32)
    kernel = depth_weight.astype(jnp.float32)
    conv = depthwise(padded, kernel, local_frames)
    normed_conv, inverse_conv = normalize(conv)
    gained = normed_conv * depth_gain
    sig_two = jax.nn.sigmoid(gained)
    act = (gained * sig_two * keep).astype(jnp.bfloat16)
    mixed = times_transposed(act, whole_out)
    output = (wide_in + mixed).astype(jnp.bfloat16)
    sent = jnp.bfloat16 if span <= 32 else jnp.float32
    partial_out = frame_sum(grad_out, act).astype(sent)
    rows_out = lax.psum_scatter(partial_out, "ctx", scatter_dimension=0, tiled=True)
    columns = grad_out
    grad_act = jnp.dot(
        columns,
        whole_out,
        preferred_element_type=jnp.float32,
    )
    grad_gained = grad_act * keep * (sig_two * (1.0 + gained * (1.0 - sig_two)))
    grad_conv = norm_backward(grad_gained * depth_gain, normed_conv, inverse_conv).astype(
        jnp.bfloat16
    )
    grad_pad = extended(grad_conv, (("ctx", 0),), margin).astype(jnp.float32)
    grad_glu = depthwise_back(grad_pad, kernel, local_frames) * keep
    grad_wide = grad_conv.astype(jnp.float32)
    depth_local = jnp.stack(
        [
            jnp.sum(grad_wide * padded[offset : offset + local_frames], axis=0)
            for offset in range(taps)
        ],
        axis=0,
    )
    grad_projected = jnp.concatenate(
        [grad_glu * sigma, grad_glu * linear * sigma * (1.0 - sigma)], axis=1
    ).astype(jnp.bfloat16)
    partial_in = frame_sum(grad_projected, scaled_in).astype(sent)
    columns = grad_projected
    grad_scaled = jnp.dot(
        columns, whole_in, preferred_element_type=jnp.float32
    )
    grad_in = norm_backward(grad_scaled * norm_gain, normed_in, inverse_in)
    gains_local = jnp.stack(
        [jnp.sum(grad_scaled * normed_in, axis=0), jnp.sum(grad_gained * normed_conv, axis=0)],
        axis=0,
    )
    blank = jnp.zeros((-(taps + 2) % 16, width), jnp.float32)
    small = jnp.concatenate([depth_local, gains_local, blank], axis=0)
    rows_in, small = reduce_rows(partial_in, small, span)
    grad_w_in = rows_in * scale
    grad_w_out = rows_out.astype(jnp.float32) * scale
    depth_total, gains_total = small[:taps].T, small[taps : taps + 2]
    grad_local = (grad_out.astype(jnp.float32) + grad_in).astype(jnp.bfloat16)
    grad_frames = lax.all_to_all(
        grad_local.reshape(frames.shape), "ctx", split_axis=0, concat_axis=0, tiled=True
    )
    return (output, grad_frames, grad_w_in, grad_w_out, depth_total * scale, gains_total * scale)


def solution(mesh):
    placed = (
        P("groups", "ctx", None),
        P(("groups", "ctx"), None),
        P("groups"),
        P(),
        P("ctx", None),
        P(),
        P(),
        P("ctx", None),
    )
    return jax.shard_map(
        shards,
        mesh=mesh,
        in_specs=placed,
        out_specs=(
            P(("groups", "ctx"), None),
            P("groups", "ctx", None),
            P(("groups", "ctx"), None),
            P(("groups", "ctx"), None),
            P("groups", None),
            P("groups", None),
        ),
        check_vma=False,
    )
```
